32 devices in a mesh: chan: 4 (over y, x), blk: 8 (over z, core).
Axes of the slice: x: 2, y: 2, z: 4, core: 2. Of those that a mesh axis runs over, the one named last changes fastest.
Arguments:
- coeffs: bfloat16 [12, 2, 3072, 1536], P('chan', None, 'blk'), may hold values from -0.15 to 0.15
- legendre: bfloat16 [4, 768, 256, 1536], P('chan', 'blk'), may hold values from -0.15625 to 0.15625
- m_order: int32 [3072], replicated, may hold values from 0 to 3071, as said below
- sector_len: int32 [512, 16], P(('chan', 'blk')), may hold values from 256 to 4352, as said below
Outputs:
- ilc_map: float32 [512, 8192], P(('chan', 'blk'))
The draws below stay inside these ranges and needn't reach their ends.
Inputs may be any that keep to these rules, and one draw needn't show every extreme that they name: `m_order`: a permutation of 0 to 3071; slots 2 j and 2 j + 1 hold the orders m and 3071 - m. `sector_len`: the 16 lengths of each cycle sum to 8192.
All inputs are finite; a program needn't handle non-finite values.
Results may differ from the reference program's by a relative error of at most 0.0003.
Values may be sent and summed in bfloat16 or wider, within the bound.
A program may use at most 512 MiB of HBM per device.

```python
import jax
import jax.numpy as jnp
from jax import lax

CH = 12
M = 3072
LB = 1536
PIX = 8192
NSEC = 16
RN = 256
GROUPS = 4
N_CHAN = 4
N_BLK = 8


def draw_coeffs(key, part):
    shape_all = (CH, 2, M, LB)
    common_key = jax.random.fold_in(key, 101)
    noise_key = jax.random.fold_in(key, 202)
    spread_key = jax.random.fold_in(key, 303)
    common = jax.random.truncated_normal(common_key, -4.0, 4.0, (1, 2, M, LB), jnp.float32)
    noise_part = jax.random.truncated_normal(noise_key, -4.0, 4.0, shape_all, jnp.float32)
    spread = jnp.exp(jax.random.uniform(spread_key, (CH, 1, 1, 1), jnp.float32, -0.6931472, 0.6931472))
    return (0.0125 * (common + spread * noise_part)).astype(jnp.bfloat16)


def draw_m_order(key, part):
    pair_low = jax.random.permutation(key, M // 2).astype(jnp.int32)
    return jnp.stack([pair_low, M - 1 - pair_low], axis=1).reshape(M).astype(jnp.int32)


def draw_sector_len(key, part):
    cycle_count = 2 * RN
    spare_pixels = PIX // 2
    least_length = PIX // (2 * NSEC)
    inner_cuts = jax.random.randint(jax.random.fold_in(key, 7), (cycle_count, NSEC - 2), 0, spare_pixels + 1, dtype=jnp.int32)
    keep_rows = (jnp.arange(cycle_count, dtype=jnp.int32) > 0).astype(jnp.int32)
    inner_cuts = inner_cuts * keep_rows[:, None]
    cut_points = jnp.sort(jnp.concatenate([jnp.zeros((cycle_count, 1), jnp.int32), inner_cuts], axis=1), axis=1)
    bounds = jnp.concatenate([cut_points, jnp.full((cycle_count, 1), spare_pixels, jnp.int32)], axis=1)
    extra_pixels = bounds - jnp.concatenate([jnp.zeros((cycle_count, 1), jnp.int32), bounds[:, :-1]], axis=1)
    lengths = least_length + extra_pixels
    offset = jax.random.randint(jax.random.fold_in(key, 9), (cycle_count, 1), 0, NSEC, dtype=jnp.int32)
    rotation = (jnp.arange(NSEC, dtype=jnp.int32)[None, :] + offset) % NSEC
    return jnp.take_along_axis(lengths, rotation, axis=1).astype(jnp.int32)


def block_levels(rng, shape, split, smallest, high):
    gain, own = 1.0, jax.random.fold_in(rng, 6)
    for axis_at, shards_of in split:
        draws = jnp.exp(jax.random.uniform(jax.random.fold_in(own, axis_at), (shards_of,), jnp.float32, smallest / len(split), high / len(split)))
        gain = gain * jnp.repeat(draws, shape[axis_at] // shards_of).reshape([-1 if axis == axis_at else 1 for axis in range(len(shape))])
    return gain


def normal_values(key, extent, deviation, limit, split=(), kind=jnp.bfloat16):
    values = deviation * jax.random.normal(key, extent, jnp.float32)
    if split:
        values = values * block_levels(key, extent, split, -0.22, 0.18)
    return jnp.clip(values, -limit, limit).astype(kind)


def setup_inputs(seed: int = 0) -> dict:
    streams_of = jax.random.split(jax.random.key(seed), 5)
    coeffs = draw_coeffs(jax.random.fold_in(streams_of[4], 71), 0)
    legendre = normal_values(streams_of[1], (GROUPS, M // GROUPS, RN, LB), LB ** -0.5, 0.15625, ((0, 4), (1, 8)))
    m_order = draw_m_order(jax.random.fold_in(streams_of[4], 71), 0)
    sector_len = draw_sector_len(jax.random.fold_in(streams_of[4], 71), 0)
    return {"coeffs": coeffs, "legendre": legendre, "m_order": m_order, "sector_len": sector_len}


RIDGE_FACTOR = 0.05
TWO_PI = 6.283185307179586

def legendre_block(coeff_block, operator, orders):
    highest = lax.Precision.HIGHEST
    degree = M - LB + lax.iota(jnp.int32, LB)
    valid_mask = degree[None, :] >= orders[:, None]
    odd_mask = (degree[None, :] + orders[:, None]) % 2 == 1
    zero_value = jnp.zeros((), coeff_block.dtype)
    even_part = jnp.where((valid_mask & ~odd_mask)[None, None], coeff_block, zero_value)
    odd_part = jnp.where((valid_mask & odd_mask)[None, None], coeff_block, zero_value)
    operator_wide = operator.astype(jnp.float32)
    even_sum = jnp.einsum('cpsl,srl->cprs', even_part.astype(jnp.float32), operator_wide, precision=highest)
    odd_sum = jnp.einsum('cpsl,srl->cprs', odd_part.astype(jnp.float32), operator_wide, precision=highest)
    return jnp.concatenate([even_sum + odd_sum, even_sum - odd_sum], axis=2)

def cycle_synthesis(spectra, orders):
    highest = lax.Precision.HIGHEST
    order_count = spectra.shape[-1]
    fine_count = 128
    coarse_count = PIX // fine_count
    coarse_phase = (lax.iota(jnp.int32, coarse_count) * fine_count)[:, None] * orders[None, :] % PIX
    fine_phase = orders[:, None] * lax.iota(jnp.int32, fine_count)[None, :] % PIX
    coarse_angle = coarse_phase.astype(jnp.float32) * (TWO_PI / PIX)
    fine_angle = fine_phase.astype(jnp.float32) * (TWO_PI / PIX)
    weight = jnp.where(orders == 0, 1.0, 2.0).astype(jnp.float32)
    coarse_cos = jnp.cos(coarse_angle)
    coarse_sin = jnp.sin(coarse_angle)
    fine_cos = weight[:, None] * jnp.cos(fine_angle)
    fine_sin = weight[:, None] * jnp.sin(fine_angle)
    real_part = spectra[:, 0].reshape(-1, 1, order_count)
    imag_part = spectra[:, 1].reshape(-1, 1, order_count)
    shifted_real = (real_part * coarse_cos[None] - imag_part * coarse_sin[None]).reshape(-1, order_count)
    shifted_imag = (real_part * coarse_sin[None] + imag_part * coarse_cos[None]).reshape(-1, order_count)
    result = jnp.dot(shifted_real.astype(jnp.float32), fine_cos.astype(jnp.float32), precision=highest, preferred_element_type=jnp.float32)
    result = result - jnp.dot(shifted_imag.astype(jnp.float32), fine_sin.astype(jnp.float32), precision=highest, preferred_element_type=jnp.float32)
    return result.reshape(spectra.shape[0], spectra.shape[2], PIX)

def cycle_combine(cycle_map, lengths):
    highest = lax.Precision.HIGHEST
    channel_count = cycle_map.shape[0]
    sector_end = jnp.cumsum(lengths).astype(jnp.int32)
    sector_start = (sector_end - lengths).astype(jnp.int32)
    pixels = lax.iota(jnp.int32, PIX)
    member = ((pixels[None, :] >= sector_start[:, None]) & (pixels[None, :] < sector_end[:, None])).astype(jnp.float32)
    products = (cycle_map[:, None, :] * cycle_map[None, :, :]).reshape(channel_count * channel_count, PIX)
    moments = jnp.einsum('qx,kx->kq', products, member, precision=highest)
    covariance = moments.reshape(-1, channel_count, channel_count) / lengths.astype(jnp.float32)[:, None, None]
    trace_part = jnp.trace(covariance, axis1=1, axis2=2) * (RIDGE_FACTOR / channel_count)
    regular = covariance + trace_part[:, None, None] * jnp.eye(channel_count, dtype=jnp.float32)
    factor = jnp.linalg.cholesky(regular)
    unit_rhs = jnp.ones((covariance.shape[0], channel_count, 1), jnp.float32)
    forward = lax.linalg.triangular_solve(factor, unit_rhs, left_side=True, lower=True)
    solved = lax.linalg.triangular_solve(factor, forward, left_side=True, lower=True, transpose_a=True)[:, :, 0]
    weights = solved / jnp.sum(solved, axis=1, keepdims=True)
    pixel_weights = jnp.einsum('ka,kx->ax', weights, member, precision=highest)
    return jnp.sum(pixel_weights * cycle_map, axis=0)

def reference(coeffs, legendre, m_order, sector_len):
    slot_count = M // (N_CHAN * N_BLK)
    block_span = N_CHAN * slot_count

    def one_block(block_number):
        coeff_block = lax.dynamic_slice_in_dim(coeffs, block_number * block_span, block_span, 2)
        operator = lax.dynamic_slice_in_dim(legendre, block_number * slot_count, slot_count, 1)
        operator = operator.reshape(block_span, RN, LB)
        orders = lax.dynamic_slice_in_dim(m_order, block_number * block_span, block_span, 0)
        return legendre_block(coeff_block, operator, orders)
    blocks = lax.map(one_block, jnp.arange(N_BLK, dtype=jnp.int32))
    spectra = jnp.moveaxis(blocks, 0, 3).reshape(CH, 2, 2 * RN, M)
    cycle_maps = lax.map(lambda channel: cycle_synthesis(channel[None], m_order)[0], spectra)
    return lax.map(lambda cycle_pair: cycle_combine(cycle_pair[0], cycle_pair[1]), (jnp.moveaxis(cycle_maps, 1, 0), sector_len))
```

```python
import functools

import jax
import jax.numpy as jnp
from jax import lax
from jax.experimental import pallas as pl
from jax.experimental.pallas import tpu as pltpu
from jax.sharding import PartitionSpec as P

PIX = 8192
LOW = 128
HIGH = PIX // LOW
CHUNK = 1024
GROUP_ROWS = 16
RIDGE_FACTOR = 0.05
TWO_PI = 6.283185307179586


def permute_kernel(order_ref, real_in, imag_in, real_out, imag_out):
    def step(slot, carry):
        target = order_ref[slot]
        real_out[pl.ds(target, 1), :] = real_in[pl.ds(slot, 1), :]
        imag_out[pl.ds(target, 1), :] = imag_in[pl.ds(slot, 1), :]
        return carry

    lax.fori_loop(0, real_in.shape[0], step, 0, unroll=8)


def sort_orders(orders, real_rows, imag_rows):
    whole = pl.BlockSpec(real_rows.shape, lambda i, order: (0, 0))
    return pl.pallas_call(
        permute_kernel,
        grid_spec=pltpu.PrefetchScalarGridSpec(
            num_scalar_prefetch=1, grid=(1,), in_specs=[whole, whole], out_specs=[whole, whole]
        ),
        out_shape=[jax.ShapeDtypeStruct(real_rows.shape, jnp.float32)] * 2,
        compiler_params=pltpu.CompilerParams(vmem_limit_bytes=48 << 20),
    )(orders, real_rows, imag_rows)


def member_of(start, end, base, count):
    place = lax.broadcasted_iota(jnp.int32, (start.shape[0], count), 1) + base
    pixel = (place % LOW) * HIGH + place // LOW
    return (pixel >= start) & (pixel < end)


def synthesis_kernel(
    channels, shifts, x_ref, d_ref, e_ref, tc_ref, ts_ref, start_ref, end_ref,
    map_ref, moment_ref, z_ref, m_ref, p_ref,
):
    highest = lax.Precision.HIGHEST
    first = jnp.dot(d_ref[...], x_ref[0], precision=highest, preferred_element_type=jnp.float32)
    cos_turn = tc_ref[...]
    sin_turn = ts_ref[...]
    for c in range(channels):
        real = first[:HIGH, c * LOW : (c + 1) * LOW]
        imag = first[HIGH:, c * LOW : (c + 1) * LOW]
        z_ref[c * HIGH : (c + 1) * HIGH, :LOW] = real * cos_turn - imag * sin_turn
        z_ref[c * HIGH : (c + 1) * HIGH, LOW:] = real * sin_turn + imag * cos_turn
    m_ref[...] = jnp.dot(
        z_ref[...], e_ref[...], precision=highest, preferred_element_type=jnp.float32
    )
    for x2 in range(HIGH):
        map_ref[0, :, x2 * LOW : (x2 + 1) * LOW] = m_ref[pl.ds(x2, channels, stride=HIGH), :]
    p_ref[...] = jnp.zeros_like(p_ref)
    start = start_ref[0]
    end = end_ref[0]
    total = jnp.zeros((2 * shifts * GROUP_ROWS, start.shape[0]), jnp.float32)
    for chunk in range(PIX // CHUNK):
        base = chunk * CHUNK
        values = map_ref[0, :, base : base + CHUNK]
        twice = jnp.concatenate([values, values], axis=0)
        for d in range(shifts):
            p_ref[d * GROUP_ROWS : d * GROUP_ROWS + channels, :] = (
                values * twice[d : d + channels]
            )
        product = p_ref[...]
        upper = product.astype(jnp.bfloat16)
        lower = (product - upper.astype(jnp.float32)).astype(jnp.bfloat16)
        member = jnp.where(member_of(start, end, base, CHUNK), 1.0, 0.0).astype(jnp.bfloat16)
        total += lax.dot_general(
            jnp.concatenate([upper, lower], axis=0), member,
            (((1,), (1,)), ((), ())), preferred_element_type=jnp.float32,
        )
    half = shifts * GROUP_ROWS
    moment_ref[0] = total[:half] + total[half:]


def solve_kernel(channels, cov_ref, len_ref, w_ref):
    scale = 1.0 / len_ref[...].astype(jnp.float32)

    def entry(a, b):
        shift = (b - a) % channels
        row = a
        if shift > channels // 2:
            shift, row = channels - shift, b
        return cov_ref[pl.ds(shift * channels + row, 1), :] * scale

    full = {(a, b): entry(a, b) for a in range(channels) for b in range(a, channels)}
    trace = full[0, 0]
    for a in range(1, channels):
        trace = trace + full[a, a]
    ridge = trace * (RIDGE_FACTOR / channels)
    for a in range(channels):
        full[a, a] = full[a, a] + ridge
    rhs = [jnp.ones_like(scale) for _ in range(channels)]
    inverse = []
    for a in range(channels):
        inverse.append(1.0 / full[a, a])
        for b in range(a + 1, channels):
            factor = full[a, b] * inverse[a]
            for c in range(b, channels):
                full[b, c] = full[b, c] - factor * full[a, c]
            rhs[b] = rhs[b] - factor * rhs[a]
    solved = [None] * channels
    for a in reversed(range(channels)):
        value = rhs[a]
        for b in range(a + 1, channels):
            value = value - full[a, b] * solved[b]
        solved[a] = value * inverse[a]
    total = solved[0]
    for a in range(1, channels):
        total = total + solved[a]
    for a in range(channels):
        w_ref[pl.ds(a, 1), :] = solved[a] / total


def combine_kernel(map_ref, w_ref, start_ref, end_ref, out_ref):
    start = start_ref[0]
    end = end_ref[0]
    for chunk in range(PIX // CHUNK):
        base = chunk * CHUNK
        member = jnp.where(member_of(start, end, base, CHUNK), 1.0, 0.0).astype(jnp.float32)
        pixel_weights = jnp.dot(
            w_ref[0], member, precision=lax.Precision.HIGHEST,
            preferred_element_type=jnp.float32,
        )
        out_ref[0, :, base : base + CHUNK] = jnp.sum(
            pixel_weights * map_ref[0, :, base : base + CHUNK], axis=0, keepdims=True
        )


def angles(left, right, period):
    phase = left[:, None] * right[None, :] % period
    turned = phase.astype(jnp.float32) * (TWO_PI / period)
    return jnp.cos(turned), jnp.sin(turned)


def synthesize(real, imag, channels, cycles, sector_len):
    order_count = real.shape[0]
    digits = order_count // LOW
    sectors = sector_len.shape[1]
    weight = jnp.where(lax.iota(jnp.int32, order_count) == 0, 1.0, 2.0).astype(jnp.float32)
    parts = jnp.stack([real, imag]) * weight[None, :, None]
    parts = parts.reshape(2, digits, LOW, channels, cycles).transpose(4, 0, 1, 3, 2)
    parts = parts.reshape(cycles, 2 * digits, channels * LOW)
    x_low = lax.iota(jnp.int32, HIGH)
    m_low = lax.iota(jnp.int32, LOW)
    cos_d, sin_d = angles(x_low, lax.iota(jnp.int32, digits), HIGH)
    first = jnp.concatenate(
        [jnp.concatenate([cos_d, -sin_d], 1), jnp.concatenate([sin_d, cos_d], 1)], 0
    )
    cos_t, sin_t = angles(x_low, m_low, PIX)
    cos_e, sin_e = angles(m_low, m_low, LOW)
    second = jnp.concatenate([cos_e, -sin_e], 0)
    ends = jnp.cumsum(sector_len, axis=1).astype(jnp.int32)
    starts = (ends - sector_len)[:, :, None]
    ends = ends[:, :, None]
    shifts = channels // 2 + 1
    half = shifts * GROUP_ROWS

    def fixed(array):
        return pl.BlockSpec(array.shape, lambda i: (0, 0))

    def each(rows, columns):
        return pl.BlockSpec((1, rows, columns), lambda i: (i, 0, 0))

    maps, moments = pl.pallas_call(
        functools.partial(synthesis_kernel, channels, shifts),
        grid=(cycles,),
        in_specs=[
            each(2 * digits, channels * LOW), fixed(first), fixed(second), fixed(cos_t),
            fixed(sin_t), each(sectors, 1), each(sectors, 1),
        ],
        out_specs=[each(channels, PIX), each(half, sectors)],
        out_shape=[
            jax.ShapeDtypeStruct((cycles, channels, PIX), jnp.float32),
            jax.ShapeDtypeStruct((cycles, half, sectors), jnp.float32),
        ],
        scratch_shapes=[
            pltpu.VMEM((channels * HIGH, 2 * LOW), jnp.float32),
            pltpu.VMEM((channels * HIGH, LOW), jnp.float32),
            pltpu.VMEM((half, CHUNK), jnp.float32),
        ],
        compiler_params=pltpu.CompilerParams(vmem_limit_bytes=48 << 20),
    )(parts, first, second, cos_t, sin_t, starts, ends)
    covariance = moments.reshape(cycles, shifts, GROUP_ROWS, sectors)[:, :, :channels]
    covariance = covariance.transpose(1, 2, 0, 3).reshape(shifts * channels, cycles * sectors)
    weights = pl.pallas_call(
        functools.partial(solve_kernel, channels),
        out_shape=jax.ShapeDtypeStruct((channels, cycles * sectors), jnp.float32),
    )(covariance, sector_len.reshape(1, cycles * sectors))
    weights = weights.reshape(channels, cycles, sectors).transpose(1, 0, 2)
    combined = pl.pallas_call(
        combine_kernel,
        grid=(cycles,),
        in_specs=[each(channels, PIX), each(channels, sectors), each(sectors, 1), each(sectors, 1)],
        out_specs=each(1, PIX),
        out_shape=jax.ShapeDtypeStruct((cycles, 1, PIX), jnp.float32),
    )(maps, weights, starts, ends)
    return combined.reshape(cycles, HIGH, LOW).transpose(0, 2, 1).reshape(cycles, PIX)


def per_device(coeffs, legendre, m_order, sector_len):
    slot_count, north_count, degree_count = legendre.shape[1:]
    order_count = m_order.shape[0]
    group_count = lax.axis_size("chan")
    block_count = lax.axis_size("blk")
    device_count = group_count * block_count
    channels = coeffs.shape[0] * group_count
    cycles = sector_len.shape[0]
    first_slot = (lax.axis_index("blk") * group_count + lax.axis_index("chan")) * slot_count
    orders = lax.dynamic_slice_in_dim(m_order, first_slot, slot_count, 0)
    operator = legendre[0]
    degree = order_count - degree_count + lax.iota(jnp.int32, degree_count)
    valid_mask = degree[None, :] >= orders[:, None]
    parity = (degree[None, :] + orders[:, None]) % 2
    keep = jnp.stack([valid_mask & (parity == 0), valid_mask & (parity == 1)])
    zero_value = jnp.zeros((), coeffs.dtype)
    order_joined = (
        m_order.reshape(block_count, group_count, slot_count).transpose(1, 0, 2).reshape(-1)
    )
    received = []
    for p in range(2):
        part = lax.all_to_all(coeffs[:, p], "chan", split_axis=1, concat_axis=0, tiled=True)
        masked = jnp.where(keep[:, None], part[None], zero_value)
        sums = jnp.einsum("ecsl,srl->secr", masked, operator, preferred_element_type=jnp.float32)
        even_sum, odd_sum = sums[:, 0], sums[:, 1]
        spectra = jnp.concatenate([even_sum + odd_sum, even_sum - odd_sum], axis=2)
        spectra = spectra.reshape(slot_count, channels, device_count, cycles)
        spectra = spectra.transpose(2, 0, 1, 3).reshape(
            device_count, slot_count, channels * cycles
        )
        spectra = lax.all_to_all(
            spectra, ("chan", "blk"), split_axis=0, concat_axis=0, tiled=True
        )
        received.append(spectra.reshape(order_count, channels * cycles))
    real, imag = sort_orders(order_joined, received[0], received[1])
    return synthesize(real, imag, channels, cycles, sector_len)


def solution(mesh):
    placed = (
        P("chan", None, "blk", None),
        P("chan", "blk", None, None),
        P(),
        P(("chan", "blk"), None),
    )
    return jax.shard_map(
        per_device, mesh=mesh, in_specs=placed, out_specs=P(("chan", "blk"), None), check_vma=False
    )
```

```python
import functools

import jax
import jax.numpy as jnp
from jax import lax
from jax.experimental import pallas as pl
from jax.experimental.pallas import tpu as pltpu
from jax.sharding import PartitionSpec as P

PIX = 8192
LOW = 128
HIGH = PIX // LOW
CHUNK = 1024
GROUP_ROWS = 16
RIDGE_FACTOR = 0.05
TWO_PI = 6.283185307179586


def permute_kernel(order_ref, rows_in, rows_out):
    def step(slot, carry):
        rows_out[pl.ds(order_ref[slot], 1), :] = rows_in[pl.ds(slot, 1), :]
        return carry

    lax.fori_loop(0, rows_in.shape[0], step, 0, unroll=8)


def sort_orders(orders, rows):
    whole = pl.BlockSpec(rows.shape, lambda i, order: (0, 0))
    return pl.pallas_call(
        permute_kernel,
        grid_spec=pltpu.PrefetchScalarGridSpec(
            num_scalar_prefetch=1, grid=(1,), in_specs=[whole], out_specs=whole
        ),
        out_shape=jax.ShapeDtypeStruct(rows.shape, jnp.float32),
        compiler_params=pltpu.CompilerParams(vmem_limit_bytes=32 << 20),
    )(orders, rows)


def halves(value):
    upper = value.astype(jnp.bfloat16)
    return upper, (value - upper.astype(jnp.float32)).astype(jnp.bfloat16)


def split_dot(left, right):
    left_upper, left_lower = halves(left)
    right_upper, right_lower = halves(right)
    return jnp.dot(
        jnp.concatenate([left_upper, left_upper, left_lower], axis=1),
        jnp.concatenate([right_upper, right_lower, right_upper], axis=0),
        preferred_element_type=jnp.float32,
    )


def member_of(start, end, base, count):
    place = lax.broadcasted_iota(jnp.int32, (start.shape[0], count), 1) + base
    pixel = (place % LOW) * HIGH + place // LOW
    return (pixel >= start) & (pixel < end)


def synthesis_kernel(
    channels, shifts, real_ref, imag_ref, d_ref, e_ref, tc_ref, ts_ref, start_ref, end_ref,
    map_ref, moment_ref, z_ref, m_ref, p_ref,
):
    first = split_dot(d_ref[...], jnp.concatenate([real_ref[0], imag_ref[0]], axis=0))
    cos_turn = tc_ref[...]
    sin_turn = ts_ref[...]
    for c in range(channels):
        real = first[:HIGH, c * LOW : (c + 1) * LOW]
        imag = first[HIGH:, c * LOW : (c + 1) * LOW]
        z_ref[c * HIGH : (c + 1) * HIGH, :LOW] = real * cos_turn - imag * sin_turn
        z_ref[c * HIGH : (c + 1) * HIGH, LOW:] = real * sin_turn + imag * cos_turn
    m_ref[...] = split_dot(z_ref[...], e_ref[...])
    for x2 in range(HIGH):
        map_ref[0, :, x2 * LOW : (x2 + 1) * LOW] = m_ref[pl.ds(x2, channels, stride=HIGH), :]
    p_ref[...] = jnp.zeros_like(p_ref)
    start = start_ref[0]
    end = end_ref[0]
    total = jnp.zeros((2 * shifts * GROUP_ROWS, start.shape[0]), jnp.float32)
    for chunk in range(PIX // CHUNK):
        base = chunk * CHUNK
        values = map_ref[0, :, base : base + CHUNK]
        twice = jnp.concatenate([values, values], axis=0)
        for d in range(shifts):
            p_ref[d * GROUP_ROWS : d * GROUP_ROWS + channels, :] = (
                values * twice[d : d + channels]
            )
        product = p_ref[...]
        upper, lower = halves(product)
        member = jnp.where(member_of(start, end, base, CHUNK), 1.0, 0.0).astype(jnp.bfloat16)
        total += lax.dot_general(
            jnp.concatenate([upper, lower], axis=0), member,
            (((1,), (1,)), ((), ())), preferred_element_type=jnp.float32,
        )
    half = shifts * GROUP_ROWS
    moment_ref[0] = total[:half] + total[half:]


def solve_kernel(channels, cov_ref, len_ref, w_ref):
    scale = 1.0 / len_ref[...].astype(jnp.float32)

    def entry(a, b):
        shift = (b - a) % channels
        row = a
        if shift > channels // 2:
            shift, row = channels - shift, b
        return cov_ref[pl.ds(shift * channels + row, 1), :] * scale

    full = {(a, b): entry(a, b) for a in range(channels) for b in range(a, channels)}
    trace = full[0, 0]
    for a in range(1, channels):
        trace = trace + full[a, a]
    ridge = trace * (RIDGE_FACTOR / channels)
    for a in range(channels):
        full[a, a] = full[a, a] + ridge
    rhs = [jnp.ones_like(scale) for _ in range(channels)]
    inverse = []
    for a in range(channels):
        inverse.append(1.0 / full[a, a])
        for b in range(a + 1, channels):
            factor = full[a, b] * inverse[a]
            for c in range(b, channels):
                full[b, c] = full[b, c] - factor * full[a, c]
            rhs[b] = rhs[b] - factor * rhs[a]
    solved = [None] * channels
    for a in reversed(range(channels)):
        value = rhs[a]
        for b in range(a + 1, channels):
            value = value - full[a, b] * solved[b]
        solved[a] = value * inverse[a]
    total = solved[0]
    for a in range(1, channels):
        total = total + solved[a]
    for a in range(channels):
        w_ref[pl.ds(a, 1), :] = solved[a] / total


def combine_kernel(map_ref, w_ref, start_ref, end_ref, out_ref):
    start = start_ref[0]
    end = end_ref[0]
    weights = w_ref[0]
    upper, middle = halves(weights)
    lower = weights - upper.astype(jnp.float32) - middle.astype(jnp.float32)
    pieces = jnp.concatenate([upper, middle, lower.astype(jnp.bfloat16)], axis=1)
    for chunk in range(PIX // CHUNK):
        base = chunk * CHUNK
        member = jnp.where(member_of(start, end, base, CHUNK), 1.0, 0.0).astype(jnp.bfloat16)
        pixel_weights = jnp.dot(
            pieces, jnp.concatenate([member, member, member], axis=0),
            preferred_element_type=jnp.float32,
        )
        out_ref[0, :, base : base + CHUNK] = jnp.sum(
            pixel_weights * map_ref[0, :, base : base + CHUNK], axis=0, keepdims=True
        )


def angles(left, right, period):
    phase = left[:, None] * right[None, :] % period
    turned = phase.astype(jnp.float32) * (TWO_PI / period)
    return jnp.cos(turned), jnp.sin(turned)


def synthesize(real, imag, channels, cycles, sector_len):
    order_count = real.shape[0]
    digits = order_count // LOW
    sectors = sector_len.shape[1]
    weight = jnp.where(lax.iota(jnp.int32, order_count) == 0, 1.0, 2.0).astype(jnp.float32)

    def by_cycle(rows):
        rows = (rows * weight[:, None]).reshape(digits, LOW, channels, cycles)
        return rows.transpose(3, 0, 2, 1).reshape(cycles, digits, channels * LOW)

    x_low = lax.iota(jnp.int32, HIGH)
    m_low = lax.iota(jnp.int32, LOW)
    cos_d, sin_d = angles(x_low, lax.iota(jnp.int32, digits), HIGH)
    first = jnp.concatenate(
        [jnp.concatenate([cos_d, -sin_d], 1), jnp.concatenate([sin_d, cos_d], 1)], 0
    )
    cos_t, sin_t = angles(x_low, m_low, PIX)
    cos_e, sin_e = angles(m_low, m_low, LOW)
    second = jnp.concatenate([cos_e, -sin_e], 0)
    ends = jnp.cumsum(sector_len, axis=1).astype(jnp.int32)
    starts = (ends - sector_len)[:, :, None]
    ends = ends[:, :, None]
    shifts = channels // 2 + 1
    half = shifts * GROUP_ROWS

    def fixed(array):
        return pl.BlockSpec(array.shape, lambda i: (0, 0))

    def each(rows, columns):
        return pl.BlockSpec((1, rows, columns), lambda i: (i, 0, 0))

    maps, moments = pl.pallas_call(
        functools.partial(synthesis_kernel, channels, shifts),
        grid=(cycles,),
        in_specs=[
            each(digits, channels * LOW), each(digits, channels * LOW), fixed(first), fixed(second), fixed(cos_t),
            fixed(sin_t), each(sectors, 1), each(sectors, 1),
        ],
        out_specs=[each(channels, PIX), each(half, sectors)],
        out_shape=[
            jax.ShapeDtypeStruct((cycles, channels, PIX), jnp.float32),
            jax.ShapeDtypeStruct((cycles, half, sectors), jnp.float32),
        ],
        scratch_shapes=[
            pltpu.VMEM((channels * HIGH, 2 * LOW), jnp.float32),
            pltpu.VMEM((channels * HIGH, LOW), jnp.float32),
            pltpu.VMEM((half, CHUNK), jnp.float32),
        ],
        compiler_params=pltpu.CompilerParams(vmem_limit_bytes=48 << 20),
    )(by_cycle(real), by_cycle(imag), first, second, cos_t, sin_t, starts, ends)
    covariance = moments.reshape(cycles, shifts, GROUP_ROWS, sectors)[:, :, :channels]
    covariance = covariance.transpose(1, 2, 0, 3).reshape(shifts * channels, cycles * sectors)
    weights = pl.pallas_call(
        functools.partial(solve_kernel, channels),
        out_shape=jax.ShapeDtypeStruct((channels, cycles * sectors), jnp.float32),
    )(covariance, sector_len.reshape(1, cycles * sectors))
    weights = weights.reshape(channels, cycles, sectors).transpose(1, 0, 2)
    combined = pl.pallas_call(
        combine_kernel,
        grid=(cycles,),
        in_specs=[each(channels, PIX), each(channels, sectors), each(sectors, 1), each(sectors, 1)],
        out_specs=each(1, PIX),
        out_shape=jax.ShapeDtypeStruct((cycles, 1, PIX), jnp.float32),
    )(maps, weights, starts, ends)
    return combined.reshape(cycles, HIGH, LOW).transpose(0, 2, 1).reshape(cycles, PIX)


def per_device(coeffs, legendre, m_order, sector_len):
    slot_count, north_count, degree_count = legendre.shape[1:]
    order_count = m_order.shape[0]
    group_count = lax.axis_size("chan")
    block_count = lax.axis_size("blk")
    device_count = group_count * block_count
    channels = coeffs.shape[0] * group_count
    cycles = sector_len.shape[0]
    first_slot = (lax.axis_index("blk") * group_count + lax.axis_index("chan")) * slot_count
    orders = lax.dynamic_slice_in_dim(m_order, first_slot, slot_count, 0)
    operator = legendre[0]
    degree = order_count - degree_count + lax.iota(jnp.int32, degree_count)
    valid_mask = degree[None, :] >= orders[:, None]
    parity = (degree[None, :] + orders[:, None]) % 2
    keep = jnp.stack([valid_mask & (parity == 0), valid_mask & (parity == 1)])
    zero_value = jnp.zeros((), coeffs.dtype)
    order_joined = (
        m_order.reshape(block_count, group_count, slot_count).transpose(1, 0, 2).reshape(-1)
    )
    received = []
    for p in range(2):
        part = lax.all_to_all(coeffs[:, p], "chan", split_axis=1, concat_axis=0, tiled=True)
        masked = jnp.where(keep[:, None], part[None], zero_value)
        sums = jnp.einsum("ecsl,srl->secr", masked, operator, preferred_element_type=jnp.float32)
        even_sum, odd_sum = sums[:, 0], sums[:, 1]
        spectra = jnp.concatenate([even_sum + odd_sum, even_sum - odd_sum], axis=2)
        spectra = spectra.reshape(slot_count, channels, device_count, cycles)
        spectra = spectra.transpose(2, 0, 1, 3).reshape(
            device_count, slot_count, channels * cycles
        )
        spectra = lax.all_to_all(
            spectra, ("chan", "blk"), split_axis=0, concat_axis=0, tiled=True
        )
        received.append(
            sort_orders(order_joined, spectra.reshape(order_count, channels * cycles))
        )
    return synthesize(received[0], received[1], channels, cycles, sector_len)


def solution(mesh):
    placed = (
        P("chan", None, "blk", None),
        P("chan", "blk", None, None),
        P(),
        P(("chan", "blk"), None),
    )
    return jax.shard_map(
        per_device, mesh=mesh, in_specs=placed, out_specs=P(("chan", "blk"), None), check_vma=False
    )
```
